256 devices in a mesh: freq: 8 (over y, core), tile: 32 (over z, x).
Axes of the slice: x: 4, y: 4, z: 8, core: 2. Of those that a mesh axis runs over, the one named last changes fastest.
Arguments:
- focus_start: float32 [16, 2, 64, 8192], P('freq', None, None, 'tile'), may hold values from -6 to 6
- v_factor: bfloat16 [16, 32, 32, 64, 2, 256], P('freq', None, 'tile'), may hold values from -0.25 to 0.25
- u_factor: bfloat16 [16, 32, 32, 64, 2, 256], P('freq', 'tile'), may hold values from -0.109375 to 0.109375
- tile_ranks: int32 [16, 32, 32], P('freq'), may hold values from 8 to 64
- onsets: int32 [8192], P('tile'), may hold values from 64 to 512
Outputs:
- focusing: float32 [16, 2, 64, 8192], P('freq', None, None, 'tile')
- upgoing: float32 [16, 2, 64, 8192], P('freq', None, None, 'tile')
The draws below stay inside these ranges and needn't reach their ends.
All inputs are finite; a program needn't handle non-finite values.
Results may differ from the reference program's by a relative error of at most 0.006.
Values may be sent and summed in bfloat16 or wider, within the bound.
A program may use at most 128 MiB of HBM per device.

```python
import math
import jax
import jax.numpy as jnp
from jax import lax

TILE = 256
RANK = 64
S = 64
NT = 512
ITERS = 2
TILES = 32
NF = 16
N = 8192


def place_ends(drawn, own_key, smallest, top_value):
    index_at = [jax.random.randint(jax.random.fold_in(own_key, axis), (), 0, length) for axis, length in enumerate(drawn.shape)]
    main_axis = drawn.shape.index(max(drawn.shape))
    beside = index_at[:main_axis] + [(index_at[main_axis] + 1) % drawn.shape[main_axis]] + index_at[main_axis + 1:]
    return drawn.at[tuple(index_at)].set(smallest).at[tuple(beside)].set(top_value)


def block_scale(stream_key, dims, cuts, smallest, top_value):
    loudness, own = 1.0, jax.random.fold_in(stream_key, 6)
    for dim, blocks in cuts:
        draws = jnp.exp(jax.random.uniform(jax.random.fold_in(own, dim), (blocks,), jnp.float32, smallest / len(cuts), top_value / len(cuts)))
        loudness = loudness * jnp.repeat(draws, dims[dim] // blocks).reshape([-1 if axis == dim else 1 for axis in range(len(dims))])
    return loudness


def normal_values(own_key, extent, scale, most, pieces=(), kind=jnp.bfloat16):
    array = scale * jax.random.normal(own_key, extent, jnp.float32)
    if pieces:
        array = array * block_scale(own_key, extent, pieces, -0.22, 0.18)
    return jnp.clip(array, -most, most).astype(kind)


def setup_inputs(seed: int = 0) -> dict:
    splits = jax.random.split(jax.random.key(seed), 6)
    focus_start = normal_values(splits[0], (NF, 2, S, N), 1.0, 6.0, ((0, 8), (3, 32)), jnp.float32)
    v_factor = normal_values(splits[1], (NF, TILES, TILES, RANK, 2, TILE), (2 * TILE) ** -0.5, 0.25, ((0, 8), (2, 32)))
    u_factor = normal_values(splits[2], (NF, TILES, TILES, RANK, 2, TILE), (3 * TILES * RANK // 2) ** -0.5, 0.109375, ((0, 8), (1, 32)))
    tile_ranks = place_ends(jax.random.randint(splits[3], (NF, TILES, TILES), RANK // 8, RANK + 1), jax.random.fold_in(splits[3], 1), RANK // 8, RANK).astype(jnp.int32)
    onsets = place_ends(jax.random.randint(splits[4], (N,), NT // 8, NT + 1), jax.random.fold_in(splits[4], 1), NT // 8, NT).astype(jnp.int32)
    return {"focus_start": focus_start, "v_factor": v_factor, "u_factor": u_factor, "tile_ranks": tile_ranks, "onsets": onsets}


def fourier_table():
    samples = jnp.arange(NT, dtype=jnp.int32)
    wave_numbers = jnp.arange(NF, dtype=jnp.int32) + 1
    phases = samples[:, None] * wave_numbers[None, :] % NT
    angles = phases.astype(jnp.float32) * (2.0 * math.pi / NT)
    fourier = jnp.stack([jnp.cos(angles), jnp.sin(angles)], axis=2) * math.sqrt(2.0 / NT)
    return fourier.reshape(NT, NF * 2)

def apply_gate(signal, onsets):
    fourier = fourier_table()
    blocks = signal.reshape(NF * 2, S, TILES, TILE).transpose(2, 0, 1, 3)
    limits = onsets.reshape(TILES, TILE)

    def one_block(paired):
        piece, bounds = paired
        in_time = jnp.dot(fourier, piece.reshape(NF * 2, S * TILE), precision=lax.Precision.HIGHEST)
        window = (jnp.arange(NT)[:, None] < bounds[None, :]).astype(in_time.dtype)
        in_time = (in_time.reshape(NT, S, TILE) * window[:, None, :]).reshape(NT, S * TILE)
        return jnp.dot(fourier.T, in_time, precision=lax.Precision.HIGHEST).reshape(NF * 2, S, TILE)
    result = lax.map(one_block, (blocks, limits))
    return result.transpose(1, 2, 0, 3).reshape(NF, 2, S, TILES * TILE)

def round_half(value):
    return lax.optimization_barrier(value.astype(jnp.bfloat16)).astype(jnp.float32)

def split_parts(factor):
    return (factor[:, :, :, 0, :].astype(jnp.float32), factor[:, :, :, 1, :].astype(jnp.float32))

def rank_mask(rank_part):
    return (jnp.arange(RANK)[None, None, :] < rank_part[:, :, None]).astype(jnp.float32)[..., None]

def forward_one(packed):
    v_part, u_part, rank_part, signal = packed
    rounded = round_half(signal).reshape(2, S, TILES, TILE)
    v_real, v_imag = split_parts(v_part)
    u_real, u_imag = split_parts(u_part)
    active = rank_mask(rank_part)
    y_real = jnp.einsum('ijrt,sjt->ijrs', v_real, rounded[0]) - jnp.einsum('ijrt,sjt->ijrs', v_imag, rounded[1])
    y_imag = jnp.einsum('ijrt,sjt->ijrs', v_real, rounded[1]) + jnp.einsum('ijrt,sjt->ijrs', v_imag, rounded[0])
    y_real = round_half(y_real * active)
    y_imag = round_half(y_imag * active)
    z_real = jnp.einsum('ijrt,ijrs->ist', u_real, y_real) - jnp.einsum('ijrt,ijrs->ist', u_imag, y_imag)
    z_imag = jnp.einsum('ijrt,ijrs->ist', u_real, y_imag) + jnp.einsum('ijrt,ijrs->ist', u_imag, y_real)
    return jnp.stack([z_real, z_imag]).transpose(0, 2, 1, 3).reshape(2, S, TILES * TILE)

def backward_one(packed):
    v_part, u_part, rank_part, signal = packed
    rounded = round_half(signal).reshape(2, S, TILES, TILE)
    v_real, v_imag = split_parts(v_part)
    u_real, u_imag = split_parts(u_part)
    active = rank_mask(rank_part)
    c_real = jnp.einsum('ijrt,sit->ijrs', u_real, rounded[0]) + jnp.einsum('ijrt,sit->ijrs', u_imag, rounded[1])
    c_imag = jnp.einsum('ijrt,sit->ijrs', u_real, rounded[1]) - jnp.einsum('ijrt,sit->ijrs', u_imag, rounded[0])
    c_real = round_half(c_real * active)
    c_imag = round_half(c_imag * active)
    w_real = jnp.einsum('ijrt,ijrs->jst', v_real, c_real) + jnp.einsum('ijrt,ijrs->jst', v_imag, c_imag)
    w_imag = jnp.einsum('ijrt,ijrs->jst', v_real, c_imag) - jnp.einsum('ijrt,ijrs->jst', v_imag, c_real)
    return jnp.stack([w_real, w_imag]).transpose(0, 2, 1, 3).reshape(2, S, TILES * TILE)

def reference(focus_start, v_factor, u_factor, tile_ranks, onsets):
    signal = focus_start
    upgoing = focus_start
    for step_index in range(ITERS):
        row_image = lax.map(forward_one, (v_factor, u_factor, tile_ranks, signal))
        upgoing = apply_gate(row_image, onsets)
        returned = lax.map(backward_one, (v_factor, u_factor, tile_ranks, upgoing))
        signal = focus_start + apply_gate(returned, onsets)
    return (signal, upgoing)
```

```python
import functools
import math

import jax
import jax.numpy as jnp
import ml_dtypes
import numpy as np
from jax import lax
from jax.experimental import pallas as pl
from jax.experimental.pallas import tpu as pltpu
from jax.sharding import PartitionSpec as P

TILE = 256
RANK = 64
S = 64
NT = 512
ITERS = 2
NF = 16
ZS = 8
XS = 4
TILES = ZS * XS
GROUPS = 8
CHUNKS = 2
SC = S // CHUNKS
HALVES = 2 * ITERS
PHASES = HALVES * CHUNKS
ROWS = TILES * RANK
HALF = TILE // 2
TABLE = 48
MESH = pl.DeviceIdType.MESH
F32 = jnp.float32
BF16 = jnp.bfloat16


def trig_parts():
    orders = np.arange(TABLE)[:, None] - (NF - 1)
    angles = (orders * np.arange(NT)[None, :] % NT) * (2.0 * math.pi / NT)
    rest = np.concatenate([np.cos(angles), np.sin(angles)], axis=0)
    parts = []
    for _ in range(3):
        part = rest.astype(ml_dtypes.bfloat16)
        parts.append(part)
        rest = rest - part.astype(np.float64)
    return np.concatenate(parts, axis=0)


def contract(left, right, left_dim, right_dim):
    return lax.dot_general(
        left, right, (((left_dim,), (right_dim,)), ((), ())), preferred_element_type=F32
    )


def kernel(
    start_ref, v_hbm, u_hbm, onset_ref, trig_ref,
    focus_ref, up_ref,
    v_ref, u_ref, stack, code_out, code_in, turned,
    wave_out, wave_in, gated_out, gated_in, table, gate_rows,
    load_sem, code_send, code_recv, wave_send, wave_recv, gated_send, gated_recv,
):
    me_f = lax.axis_index("freq")
    me_t = lax.axis_index("tile")
    me_z = me_t // XS
    me_x = me_t % XS

    barrier = pltpu.get_barrier_semaphore()
    for step in range(1, GROUPS):
        pl.semaphore_signal(
            barrier, inc=1, device_id=((me_f + step) % GROUPS, me_t), device_id_type=MESH
        )
    for step in range(1, TILES):
        pl.semaphore_signal(
            barrier, inc=1, device_id=(me_f, (me_t + step) % TILES), device_id_type=MESH
        )
    load_v = pltpu.make_async_copy(v_hbm, v_ref, load_sem.at[0])
    load_u = pltpu.make_async_copy(u_hbm, u_ref, load_sem.at[1])
    load_v.start()
    load_u.start()

    def set_stack(chunk, fields, forward):
        for band in range(2):
            real = fields[band][0].astype(BF16)
            imag = fields[band][1].astype(BF16)
            top = band * 2 * SC
            if forward:
                blocks = ((real, -imag), (imag, real))
            else:
                blocks = ((real, imag), (imag, -real))
            for part in range(2):
                rows = slice(top + part * SC, top + (part + 1) * SC)
                stack[chunk, band, rows, 0:TILE] = blocks[part][0]
                stack[chunk, band, rows, TILE : 2 * TILE] = blocks[part][1]

    def send_codes(factor_ref, phase, chunk):
        def group(index, carry):
            ahead = ZS // 2 + ((index + 1) // 2) * (1 - 2 * (index % 2))
            z = (me_z + ahead) % ZS
            first = pl.multiple_of(z * (XS * RANK), XS * RANK)
            rows = pl.ds(first, XS * RANK)
            product = contract(factor_ref[0, rows, :], stack[chunk, 0], 1, 1) + contract(
                factor_ref[1, rows, :], stack[chunk, 1], 1, 1
            )
            code_out[phase, rows, :] = product.astype(BF16)
            for over in (2, 1, 3, 0):
                tile = z * XS + (me_x + over) % XS

                def start(tile=tile):
                    pltpu.make_async_remote_copy(
                        src_ref=code_out.at[phase, pl.ds(pl.multiple_of(tile * RANK, RANK), RANK)],
                        dst_ref=code_in.at[phase, pl.ds(pl.multiple_of(me_t * RANK, RANK), RANK)],
                        send_sem=code_send.at[phase],
                        recv_sem=code_recv.at[phase],
                        device_id=(me_f, tile),
                        device_id_type=MESH,
                    ).start()

                if over:
                    start()
                else:
                    pl.when(index < ZS - 1)(start)
            return carry

        lax.fori_loop(0, ZS, group, 0)
        own = pl.ds(pl.multiple_of(me_t * RANK, RANK), RANK)
        code_in[phase, own, :] = code_out[phase, own, :]

    def wait_bytes(ref, sem):
        pltpu.make_async_copy(ref, ref, sem).wait()

    def image(factor_ref, phase, forward):
        wait_bytes(code_in.at[phase, pl.ds(0, ROWS - RANK)], code_recv.at[phase])
        turned[...] = code_in[phase].T
        sign = 1.0 if forward else -1.0
        for band in range(2):
            product = contract(
                turned[band * 2 * SC : (band + 1) * 2 * SC, :], factor_ref[band], 1, 0
            )
            real = product[:SC, :TILE] - sign * product[SC:, TILE:]
            imag = product[SC:, :TILE] + sign * product[:SC, TILE:]
            for group in range(GROUPS):
                rows = slice((group // 2) * 8, (group // 2 + 1) * 8)
                lanes = slice((group % 2) * HALF, (group % 2 + 1) * HALF)
                wave_out[phase, group, band * 2] = real[rows, lanes]
                wave_out[phase, group, band * 2 + 1] = imag[rows, lanes]

    def exchange(source, target, send, recv, phase):
        for step in (4, 5, 3, 2, 6, 7, 1):
            peer = (me_f + step) % GROUPS
            pltpu.make_async_remote_copy(
                src_ref=source.at[phase, peer],
                dst_ref=target.at[phase, me_f],
                send_sem=send.at[phase],
                recv_sem=recv.at[phase],
                device_id=(peer, me_t),
                device_id_type=MESH,
            ).start()
        target[phase, me_f] = source[phase, me_f]
        wait_bytes(target.at[phase, pl.ds(0, GROUPS - 1)], recv.at[phase])

    def gate(phase):
        waves = [wave_in[phase, index // 4, index % 4] for index in range(2 * NF)]

        def row(index, carry):
            total = None
            for part in range(2):
                for wave in range(NF):
                    weight = gate_rows[index, part, wave : wave + 1, :]
                    term = weight * waves[2 * wave + part]
                    total = term if total is None else total + term
            gated_out[phase, index // 4, index % 4] = total
            return carry

        lax.fori_loop(0, 2 * NF, row, 0)

    def gated_fields(phase):
        return [
            [
                jnp.concatenate(
                    [
                        jnp.concatenate(
                            [gated_in[phase, 2 * up + side, band * 2 + part] for side in range(2)], axis=1
                        )
                        for up in range(GROUPS // 2)
                    ],
                    axis=0,
                )
                for part in range(2)
            ]
            for band in range(2)
        ]

    def start_fields(chunk):
        rows = slice(chunk * SC, (chunk + 1) * SC)
        return [[start_ref[band, part, rows, :] for part in range(2)] for band in range(2)]

    stack[...] = jnp.zeros_like(stack)
    for chunk in range(CHUNKS):
        set_stack(chunk, start_fields(chunk), True)
    load_v.wait()
    pl.semaphore_wait(barrier, GROUPS + TILES - 2)
    for chunk in range(CHUNKS):
        send_codes(v_ref, chunk, chunk)

    limits = onset_ref[pl.ds(me_f % 2, 1), :]
    window = jnp.where(lax.broadcasted_iota(jnp.int32, (NT, HALF), 0) < limits, 1.0, 0.0).astype(BF16)
    sums = contract(trig_ref[...], window, 1, 0)
    table[...] = (sums[: 2 * TABLE] + sums[2 * TABLE : 4 * TABLE] + sums[4 * TABLE :]) * (1.0 / NT)
    for wave in range(NF):
        low, high = NF - 1 - wave, NF + 1 + wave
        cos_low = table[low : low + NF, :]
        cos_high = table[high : high + NF, :]
        sin_low = table[TABLE + low : TABLE + low + NF, :]
        sin_high = table[TABLE + high : TABLE + high + NF, :]
        gate_rows[2 * wave, 0] = cos_low + cos_high
        gate_rows[2 * wave, 1] = sin_high + sin_low
        gate_rows[2 * wave + 1, 0] = sin_high - sin_low
        gate_rows[2 * wave + 1, 1] = cos_low - cos_high
    load_u.wait()

    for half in range(HALVES):
        forward = half % 2 == 0
        for chunk in range(CHUNKS):
            phase = half * CHUNKS + chunk
            rows = slice(chunk * SC, (chunk + 1) * SC)
            image(u_ref if forward else v_ref, phase, forward)
            exchange(wave_out, wave_in, wave_send, wave_recv, phase)
            gate(phase)
            exchange(gated_out, gated_in, gated_send, gated_recv, phase)
            fields = gated_fields(phase)
            if not forward:
                begun = start_fields(chunk)
                fields = [[begun[band][part] + fields[band][part] for part in range(2)] for band in range(2)]
            if half + 1 < HALVES:
                set_stack(chunk, fields, not forward)
                send_codes(u_ref if forward else v_ref, phase + CHUNKS, chunk)
            if half >= HALVES - 2:
                target = up_ref if forward else focus_ref
                for band in range(2):
                    for part in range(2):
                        target[band, part, rows, :] = fields[band][part]
    for phase in range(PHASES):
        wait_bytes(code_out.at[phase, pl.ds(0, ROWS - RANK)], code_send.at[phase])
        wait_bytes(wave_out.at[phase, pl.ds(0, GROUPS - 1)], wave_send.at[phase])
        wait_bytes(gated_out.at[phase, pl.ds(0, GROUPS - 1)], gated_send.at[phase])


def per_device(trig, focus_start, v_factor, u_factor, tile_ranks, onsets):
    own_tile = lax.axis_index("tile")
    column_ranks = lax.dynamic_slice_in_dim(tile_ranks, own_tile, 1, 2)[:, :, 0]
    row_ranks = lax.dynamic_slice_in_dim(tile_ranks, own_tile, 1, 1)[:, 0, :]
    levels = lax.iota(jnp.int32, RANK)

    def packed(factor, ranks):
        live = levels[None, None, :] < ranks[:, :, None]
        blocks = factor.reshape(2, TILES, RANK, 2, TILE)
        blocks = jnp.where(live[..., None, None], blocks, jnp.zeros_like(blocks))
        return blocks.reshape(2, ROWS, 2 * TILE)

    vmem = pl.BlockSpec(memory_space=pltpu.VMEM)
    anywhere = pl.BlockSpec(memory_space=pl.ANY)
    dma = pltpu.SemaphoreType.DMA
    field = jax.ShapeDtypeStruct((2, 2, S, TILE), F32)
    return pl.pallas_call(
        kernel,
        out_shape=(field, field),
        in_specs=[vmem, anywhere, anywhere, vmem, vmem],
        out_specs=(vmem, vmem),
        scratch_shapes=[
            pltpu.VMEM((2, ROWS, 2 * TILE), BF16),
            pltpu.VMEM((2, ROWS, 2 * TILE), BF16),
            pltpu.VMEM((CHUNKS, 2, 4 * SC, 2 * TILE), BF16),
            pltpu.VMEM((PHASES, ROWS, 4 * SC), BF16),
            pltpu.VMEM((PHASES, ROWS, 4 * SC), BF16),
            pltpu.VMEM((4 * SC, ROWS), BF16),
            pltpu.VMEM((PHASES, GROUPS, 4, 8, HALF), F32),
            pltpu.VMEM((PHASES, GROUPS, 4, 8, HALF), F32),
            pltpu.VMEM((PHASES, GROUPS, 4, 8, HALF), F32),
            pltpu.VMEM((PHASES, GROUPS, 4, 8, HALF), F32),
            pltpu.VMEM((2 * TABLE, HALF), F32),
            pltpu.VMEM((2 * NF, 2, NF, HALF), F32),
            dma((2,)),
            dma((PHASES,)),
            dma((PHASES,)),
            dma((PHASES,)),
            dma((PHASES,)),
            dma((PHASES,)),
            dma((PHASES,)),
        ],
        compiler_params=pltpu.CompilerParams(collective_id=0, has_side_effects=True),
    )(
        focus_start,
        packed(v_factor, column_ranks),
        packed(u_factor, row_ranks),
        onsets.reshape(2, HALF),
        trig,
    )


def solution(mesh):
    placed = (
        P("freq", None, None, "tile"),
        P("freq", None, "tile", None, None, None),
        P("freq", "tile", None, None, None, None),
        P("freq", None, None),
        P("tile"),
    )
    trig = trig_parts()

    def body(*args):
        return per_device(jnp.asarray(trig), *args)

    return jax.shard_map(
        body,
        mesh=mesh,
        in_specs=placed,
        out_specs=(P("freq", None, None, "tile"), P("freq", None, None, "tile")),
        check_vma=False,
    )
```

```python
import functools
import math

import jax
import jax.numpy as jnp
import ml_dtypes
import numpy as np
from jax import lax
from jax.experimental import pallas as pl
from jax.experimental.pallas import tpu as pltpu
from jax.sharding import PartitionSpec as P

TILE = 256
RANK = 64
S = 64
NT = 512
ITERS = 2
NF = 16
ZS = 8
XS = 4
TILES = ZS * XS
GROUPS = 8
CHUNKS = 2
SC = S // CHUNKS
HALVES = 2 * ITERS
PHASES = HALVES * CHUNKS
ROWS = TILES * RANK
HALF = TILE // 2
TABLE = 48
MESH = pl.DeviceIdType.MESH
F32 = jnp.float32
BF16 = jnp.bfloat16


def trig_parts():
    orders = np.arange(TABLE)[:, None] - (NF - 1)
    angles = (orders * np.arange(NT)[None, :] % NT) * (2.0 * math.pi / NT)
    rest = np.concatenate([np.cos(angles), np.sin(angles)], axis=0)
    parts = []
    for _ in range(3):
        part = rest.astype(ml_dtypes.bfloat16)
        parts.append(part)
        rest = rest - part.astype(np.float64)
    return np.concatenate(parts, axis=0)


def contract(left, right, left_dim, right_dim):
    return lax.dot_general(
        left, right, (((left_dim,), (right_dim,)), ((), ())), preferred_element_type=F32
    )


def kernel(
    start_ref, v_hbm, u_hbm, rank_ref, onset_ref, trig_ref,
    focus_ref, up_ref,
    v_raw, u_raw, v_ref, u_ref, spread, stack, code_out, code_in, turned,
    wave_out, wave_in, gated_out, gated_in, table, gate_rows,
    load_sem, code_send, code_recv, wave_send, wave_recv, gated_send, gated_recv,
):
    me_f = lax.axis_index("freq")
    me_t = lax.axis_index("tile")
    me_z = me_t // XS
    me_x = me_t % XS

    barrier = pltpu.get_barrier_semaphore()
    for step in range(1, GROUPS):
        pl.semaphore_signal(
            barrier, inc=1, device_id=((me_f + step) % GROUPS, me_t), device_id_type=MESH
        )
    for step in range(1, TILES):
        pl.semaphore_signal(
            barrier, inc=1, device_id=(me_f, (me_t + step) % TILES), device_id_type=MESH
        )
    load_v = pltpu.make_async_copy(v_hbm, v_raw, load_sem.at[0])
    load_u = pltpu.make_async_copy(u_hbm, u_raw, load_sem.at[1])
    load_v.start()
    load_u.start()

    def set_stack(chunk, fields, forward):
        for band in range(2):
            real = fields[band][0].astype(BF16)
            imag = fields[band][1].astype(BF16)
            top = band * 2 * SC
            if forward:
                blocks = ((real, -imag), (imag, real))
            else:
                blocks = ((real, imag), (imag, -real))
            for part in range(2):
                rows = slice(top + part * SC, top + (part + 1) * SC)
                stack[chunk, band, rows, 0:TILE] = blocks[part][0]
                stack[chunk, band, rows, TILE : 2 * TILE] = blocks[part][1]

    def unpack(raw, factor_ref, tile, slot, rank_of):
        for band in range(2):
            live = lax.broadcasted_iota(jnp.int32, (RANK, HALF), 0) < rank_of(band, tile)
            spread[slot, band] = raw[band, tile].astype(F32)
            rows = pl.ds(pl.multiple_of(tile * RANK, RANK), RANK)
            for side in range(2):
                for part in range(2):
                    piece = spread[slot, band, pl.ds(2 * side + part, RANK, stride=4), :]
                    piece = jnp.where(live, piece, 0.0).astype(BF16)
                    left = part * TILE + side * HALF
                    factor_ref[band, rows, left : left + HALF] = piece

    def send_codes(factor_ref, phase, chunk, prepare=None):
        def group(index, carry):
            ahead = ZS // 2 + ((index + 1) // 2) * (1 - 2 * (index % 2))
            z = (me_z + ahead) % ZS
            if prepare is not None:
                prepare(z)
            first = pl.multiple_of(z * (XS * RANK), XS * RANK)
            rows = pl.ds(first, XS * RANK)
            product = contract(factor_ref[0, rows, :], stack[chunk, 0], 1, 1) + contract(
                factor_ref[1, rows, :], stack[chunk, 1], 1, 1
            )
            code_out[phase, rows, :] = product.astype(BF16)
            for over in (2, 1, 3, 0):
                tile = z * XS + (me_x + over) % XS

                def start(tile=tile):
                    pltpu.make_async_remote_copy(
                        src_ref=code_out.at[phase, pl.ds(pl.multiple_of(tile * RANK, RANK), RANK)],
                        dst_ref=code_in.at[phase, pl.ds(pl.multiple_of(me_t * RANK, RANK), RANK)],
                        send_sem=code_send.at[phase],
                        recv_sem=code_recv.at[phase],
                        device_id=(me_f, tile),
                        device_id_type=MESH,
                    ).start()

                if over:
                    start()
                else:
                    pl.when(index < ZS - 1)(start)
            return carry

        lax.fori_loop(0, ZS, group, 0)
        own = pl.ds(pl.multiple_of(me_t * RANK, RANK), RANK)
        code_in[phase, own, :] = code_out[phase, own, :]

    def wait_bytes(ref, sem):
        pltpu.make_async_copy(ref, ref, sem).wait()

    def image(factor_ref, phase, forward):
        wait_bytes(code_in.at[phase, pl.ds(0, ROWS - RANK)], code_recv.at[phase])
        turned[...] = code_in[phase].T
        sign = 1.0 if forward else -1.0
        for band in range(2):
            product = contract(
                turned[band * 2 * SC : (band + 1) * 2 * SC, :], factor_ref[band], 1, 0
            )
            real = product[:SC, :TILE] - sign * product[SC:, TILE:]
            imag = product[SC:, :TILE] + sign * product[:SC, TILE:]
            for group in range(GROUPS):
                rows = slice((group // 2) * 8, (group // 2 + 1) * 8)
                lanes = slice((group % 2) * HALF, (group % 2 + 1) * HALF)
                wave_out[phase, group, band * 2] = real[rows, lanes]
                wave_out[phase, group, band * 2 + 1] = imag[rows, lanes]

    def exchange(source, target, send, recv, phase):
        for step in (4, 5, 3, 2, 6, 7, 1):
            peer = (me_f + step) % GROUPS
            pltpu.make_async_remote_copy(
                src_ref=source.at[phase, peer],
                dst_ref=target.at[phase, me_f],
                send_sem=send.at[phase],
                recv_sem=recv.at[phase],
                device_id=(peer, me_t),
                device_id_type=MESH,
            ).start()
        target[phase, me_f] = source[phase, me_f]
        wait_bytes(target.at[phase, pl.ds(0, GROUPS - 1)], recv.at[phase])

    def gate(phase):
        waves = [wave_in[phase, index // 4, index % 4] for index in range(2 * NF)]

        def row(index, carry):
            total = None
            for part in range(2):
                for wave in range(NF):
                    weight = gate_rows[index, part, wave : wave + 1, :]
                    term = weight * waves[2 * wave + part]
                    total = term if total is None else total + term
            gated_out[phase, index // 4, index % 4] = total
            return carry

        lax.fori_loop(0, 2 * NF, row, 0)

    def gated_fields(phase):
        return [
            [
                jnp.concatenate(
                    [
                        jnp.concatenate(
                            [gated_in[phase, 2 * up + side, band * 2 + part] for side in range(2)], axis=1
                        )
                        for up in range(GROUPS // 2)
                    ],
                    axis=0,
                )
                for part in range(2)
            ]
            for band in range(2)
        ]

    def start_fields(chunk):
        rows = slice(chunk * SC, (chunk + 1) * SC)
        return [[start_ref[band, part, rows, :] for part in range(2)] for band in range(2)]

    stack[...] = jnp.zeros_like(stack)
    for chunk in range(CHUNKS):
        set_stack(chunk, start_fields(chunk), True)
    load_v.wait()
    pl.semaphore_wait(barrier, GROUPS + TILES - 2)

    def prepare_v(z):
        for over in range(XS):
            unpack(v_raw, v_ref, z * XS + over, over, lambda band, tile: rank_ref[band, tile, me_t])

    def prepare_u(z, carry):
        for over in range(XS):
            unpack(u_raw, u_ref, z * XS + over, over, lambda band, tile: rank_ref[band, me_t, tile])
        return carry

    send_codes(v_ref, 0, 0, prepare_v)
    for chunk in range(1, CHUNKS):
        send_codes(v_ref, chunk, chunk)

    limits = onset_ref[pl.ds(me_f % 2, 1), :]
    window = jnp.where(lax.broadcasted_iota(jnp.int32, (NT, HALF), 0) < limits, 1.0, 0.0).astype(BF16)
    sums = contract(trig_ref[...], window, 1, 0)
    table[...] = (sums[: 2 * TABLE] + sums[2 * TABLE : 4 * TABLE] + sums[4 * TABLE :]) * (1.0 / NT)
    for wave in range(NF):
        low, high = NF - 1 - wave, NF + 1 + wave
        cos_low = table[low : low + NF, :]
        cos_high = table[high : high + NF, :]
        sin_low = table[TABLE + low : TABLE + low + NF, :]
        sin_high = table[TABLE + high : TABLE + high + NF, :]
        gate_rows[2 * wave, 0] = cos_low + cos_high
        gate_rows[2 * wave, 1] = sin_high + sin_low
        gate_rows[2 * wave + 1, 0] = sin_high - sin_low
        gate_rows[2 * wave + 1, 1] = cos_low - cos_high
    load_u.wait()
    lax.fori_loop(0, ZS, prepare_u, 0)

    for half in range(HALVES):
        forward = half % 2 == 0
        for chunk in range(CHUNKS):
            phase = half * CHUNKS + chunk
            rows = slice(chunk * SC, (chunk + 1) * SC)
            image(u_ref if forward else v_ref, phase, forward)
            exchange(wave_out, wave_in, wave_send, wave_recv, phase)
            gate(phase)
            exchange(gated_out, gated_in, gated_send, gated_recv, phase)
            fields = gated_fields(phase)
            if not forward:
                begun = start_fields(chunk)
                fields = [[begun[band][part] + fields[band][part] for part in range(2)] for band in range(2)]
            if half + 1 < HALVES:
                set_stack(chunk, fields, not forward)
                send_codes(u_ref if forward else v_ref, phase + CHUNKS, chunk)
            if half >= HALVES - 2:
                target = up_ref if forward else focus_ref
                for band in range(2):
                    for part in range(2):
                        target[band, part, rows, :] = fields[band][part]
    for phase in range(PHASES):
        wait_bytes(code_out.at[phase, pl.ds(0, ROWS - RANK)], code_send.at[phase])
        wait_bytes(wave_out.at[phase, pl.ds(0, GROUPS - 1)], wave_send.at[phase])
        wait_bytes(gated_out.at[phase, pl.ds(0, GROUPS - 1)], gated_send.at[phase])


def per_device(trig, focus_start, v_factor, u_factor, tile_ranks, onsets):
    def split_lanes(factor):
        blocks = factor.reshape(2, TILES, RANK, 2, 2, HALF)
        return blocks.transpose(0, 1, 2, 4, 3, 5).reshape(2, TILES, 4 * RANK, HALF)

    vmem = pl.BlockSpec(memory_space=pltpu.VMEM)
    anywhere = pl.BlockSpec(memory_space=pl.ANY)
    dma = pltpu.SemaphoreType.DMA
    field = jax.ShapeDtypeStruct((2, 2, S, TILE), F32)
    return pl.pallas_call(
        kernel,
        out_shape=(field, field),
        in_specs=[vmem, anywhere, anywhere, pl.BlockSpec(memory_space=pltpu.SMEM), vmem, vmem],
        out_specs=(vmem, vmem),
        scratch_shapes=[
            pltpu.VMEM((2, TILES, 4 * RANK, HALF), BF16),
            pltpu.VMEM((2, TILES, 4 * RANK, HALF), BF16),
            pltpu.VMEM((2, ROWS, 2 * TILE), BF16),
            pltpu.VMEM((2, ROWS, 2 * TILE), BF16),
            pltpu.VMEM((XS, 2, 4 * RANK, HALF), F32),
            pltpu.VMEM((CHUNKS, 2, 4 * SC, 2 * TILE), BF16),
            pltpu.VMEM((PHASES, ROWS, 4 * SC), BF16),
            pltpu.VMEM((PHASES, ROWS, 4 * SC), BF16),
            pltpu.VMEM((4 * SC, ROWS), BF16),
            pltpu.VMEM((PHASES, GROUPS, 4, 8, HALF), F32),
            pltpu.VMEM((PHASES, GROUPS, 4, 8, HALF), F32),
            pltpu.VMEM((PHASES, GROUPS, 4, 8, HALF), F32),
            pltpu.VMEM((PHASES, GROUPS, 4, 8, HALF), F32),
            pltpu.VMEM((2 * TABLE, HALF), F32),
            pltpu.VMEM((2 * NF, 2, NF, HALF), F32),
            dma((2,)),
            dma((PHASES,)),
            dma((PHASES,)),
            dma((PHASES,)),
            dma((PHASES,)),
            dma((PHASES,)),
            dma((PHASES,)),
        ],
        compiler_params=pltpu.CompilerParams(collective_id=0, has_side_effects=True),
    )(
        focus_start,
        split_lanes(v_factor),
        split_lanes(u_factor),
        tile_ranks,
        onsets.reshape(2, HALF),
        trig,
    )


def solution(mesh):
    placed = (
        P("freq", None, None, "tile"),
        P("freq", None, "tile", None, None, None),
        P("freq", "tile", None, None, None, None),
        P("freq", None, None),
        P("tile"),
    )
    trig = trig_parts()

    def body(*args):
        return per_device(jnp.asarray(trig), *args)

    return jax.shard_map(
        body,
        mesh=mesh,
        in_specs=placed,
        out_specs=(P("freq", None, None, "tile"), P("freq", None, None, "tile")),
        check_vma=False,
    )
```

```python
import functools
import math

import jax
import jax.numpy as jnp
import ml_dtypes
import numpy as np
from jax import lax
from jax.experimental import pallas as pl
from jax.experimental.pallas import tpu as pltpu
from jax.sharding import PartitionSpec as P

TILE = 256
RANK = 64
S = 64
NT = 512
ITERS = 2
NF = 16
ZS = 8
XS = 4
TILES = ZS * XS
GROUPS = 8
CHUNKS = 2
SC = S // CHUNKS
HALVES = 2 * ITERS
PHASES = HALVES * CHUNKS
ROWS = TILES * RANK
HALF = TILE // 2
TABLE = 48
MESH = pl.DeviceIdType.MESH
F32 = jnp.float32
BF16 = jnp.bfloat16


def trig_parts():
    orders = np.arange(TABLE)[:, None] - (NF - 1)
    angles = (orders * np.arange(NT)[None, :] % NT) * (2.0 * math.pi / NT)
    rest = np.concatenate([np.cos(angles), np.sin(angles)], axis=0)
    parts = []
    for _ in range(3):
        part = rest.astype(ml_dtypes.bfloat16)
        parts.append(part)
        rest = rest - part.astype(np.float64)
    return np.concatenate(parts, axis=0)


def contract(left, right, left_dim, right_dim):
    return lax.dot_general(
        left, right, (((left_dim,), (right_dim,)), ((), ())), preferred_element_type=F32
    )


def kernel(
    start_hbm, v_hbm, u_hbm, rank_ref, onset_ref, trig_hbm,
    focus_ref, up_ref,
    start_ref, trig_ref, v_raw, u_raw, v_ref, u_ref, spread, stack, code_out, code_in, turned,
    wave_out, wave_in, gated_out, gated_in, table, gate_rows,
    load_sem, code_send, code_recv, wave_send, wave_recv, gated_send, gated_recv,
):
    me_f = lax.axis_index("freq")
    me_t = lax.axis_index("tile")
    me_z = me_t // XS
    me_x = me_t % XS

    barrier = pltpu.get_barrier_semaphore()
    for step in range(1, GROUPS):
        pl.semaphore_signal(
            barrier, inc=1, device_id=((me_f + step) % GROUPS, me_t), device_id_type=MESH
        )
    for step in range(1, TILES):
        pl.semaphore_signal(
            barrier, inc=1, device_id=(me_f, (me_t + step) % TILES), device_id_type=MESH
        )
    load_v = pltpu.make_async_copy(v_hbm, v_raw, load_sem.at[0])
    load_u = pltpu.make_async_copy(u_hbm, u_raw, load_sem.at[1])
    load_start = pltpu.make_async_copy(start_hbm, start_ref, load_sem.at[2])
    load_trig = pltpu.make_async_copy(trig_hbm, trig_ref, load_sem.at[3])
    for load in (load_start, load_v, load_trig, load_u):
        load.start()

    def set_stack(chunk, fields, forward):
        for band in range(2):
            real = fields[band][0].astype(BF16)
            imag = fields[band][1].astype(BF16)
            top = band * 2 * SC
            if forward:
                blocks = ((real, -imag), (imag, real))
            else:
                blocks = ((real, imag), (imag, -real))
            for part in range(2):
                rows = slice(top + part * SC, top + (part + 1) * SC)
                stack[chunk, band, rows, 0:TILE] = blocks[part][0]
                stack[chunk, band, rows, TILE : 2 * TILE] = blocks[part][1]

    def unpack(raw, factor_ref, tile, slot, rank_of):
        for band in range(2):
            live = lax.broadcasted_iota(jnp.int32, (RANK, HALF), 0) < rank_of(band, tile)
            spread[slot, band] = raw[band, tile].astype(F32)
            rows = pl.ds(pl.multiple_of(tile * RANK, RANK), RANK)
            for side in range(2):
                for part in range(2):
                    piece = spread[slot, band, pl.ds(2 * side + part, RANK, stride=4), :]
                    piece = jnp.where(live, piece, 0.0).astype(BF16)
                    left = part * TILE + side * HALF
                    factor_ref[band, rows, left : left + HALF] = piece

    def send_codes(factor_ref, phase, chunk, prepare=None):
        def group(index, carry):
            ahead = ZS // 2 + ((index + 1) // 2) * (1 - 2 * (index % 2))
            z = (me_z + ahead) % ZS
            if prepare is not None:
                prepare(z)
            first = pl.multiple_of(z * (XS * RANK), XS * RANK)
            rows = pl.ds(first, XS * RANK)
            product = contract(factor_ref[0, rows, :], stack[chunk, 0], 1, 1) + contract(
                factor_ref[1, rows, :], stack[chunk, 1], 1, 1
            )
            code_out[phase, rows, :] = product.astype(BF16)
            for over in (2, 1, 3, 0):
                tile = z * XS + (me_x + over) % XS

                def start(tile=tile):
                    pltpu.make_async_remote_copy(
                        src_ref=code_out.at[phase, pl.ds(pl.multiple_of(tile * RANK, RANK), RANK)],
                        dst_ref=code_in.at[phase, pl.ds(pl.multiple_of(me_t * RANK, RANK), RANK)],
                        send_sem=code_send.at[phase],
                        recv_sem=code_recv.at[phase],
                        device_id=(me_f, tile),
                        device_id_type=MESH,
                    ).start()

                if over:
                    start()
                else:
                    pl.when(index < ZS - 1)(start)
            return carry

        lax.fori_loop(0, ZS, group, 0)
        own = pl.ds(pl.multiple_of(me_t * RANK, RANK), RANK)
        code_in[phase, own, :] = code_out[phase, own, :]

    def wait_bytes(ref, sem):
        pltpu.make_async_copy(ref, ref, sem).wait()

    def image(factor_ref, phase, forward):
        wait_bytes(code_in.at[phase, pl.ds(0, ROWS - RANK)], code_recv.at[phase])
        turned[...] = code_in[phase].T
        sign = 1.0 if forward else -1.0
        for band in range(2):
            product = contract(
                turned[band * 2 * SC : (band + 1) * 2 * SC, :], factor_ref[band], 1, 0
            )
            real = product[:SC, :TILE] - sign * product[SC:, TILE:]
            imag = product[SC:, :TILE] + sign * product[:SC, TILE:]
            for group in range(GROUPS):
                rows = slice((group // 2) * 8, (group // 2 + 1) * 8)
                lanes = slice((group % 2) * HALF, (group % 2 + 1) * HALF)
                pair = jnp.concatenate([real[rows, lanes], imag[rows, lanes]], axis=0)
                wave_out[phase, group, band] = pair.astype(BF16)

    def exchange(source, target, send, recv, phase):
        for step in (4, 5, 3, 2, 6, 7, 1):
            peer = (me_f + step) % GROUPS
            pltpu.make_async_remote_copy(
                src_ref=source.at[phase, peer],
                dst_ref=target.at[phase, me_f],
                send_sem=send.at[phase],
                recv_sem=recv.at[phase],
                device_id=(peer, me_t),
                device_id_type=MESH,
            ).start()
        target[phase, me_f] = source[phase, me_f]
        wait_bytes(target.at[phase, pl.ds(0, GROUPS - 1)], recv.at[phase])

    def gate(phase):
        waves = []
        for index in range(NF):
            pair = wave_in[phase, index // 2, index % 2].astype(F32)
            waves.append((pair[:8], pair[8:]))

        def rows(index, carry):
            results = []
            for kind in range(2):
                totals = [None] * 4
                for wave in range(NF):
                    for part in range(2):
                        weight = gate_rows[2 * index + kind, part, wave : wave + 1, :]
                        term = weight * waves[wave][part]
                        lane = 2 * (wave % 2) + part
                        totals[lane] = term if totals[lane] is None else totals[lane] + term
                results.append((totals[0] + totals[1]) + (totals[2] + totals[3]))
            gated_out[phase, index // 2, index % 2] = jnp.concatenate(results, axis=0).astype(BF16)
            return carry

        lax.fori_loop(0, NF, rows, 0)

    def gated_fields(phase):
        def field(band, part):
            part_rows = slice(part * 8, part * 8 + 8)
            bands = [
                jnp.concatenate(
                    [gated_in[phase, 2 * up + side, band].astype(F32)[part_rows] for side in range(2)], axis=1
                )
                for up in range(GROUPS // 2)
            ]
            return jnp.concatenate(bands, axis=0)

        return [[field(band, part) for part in range(2)] for band in range(2)]

    def start_fields(chunk):
        rows = slice(chunk * SC, (chunk + 1) * SC)
        return [[start_ref[band, part, rows, :] for part in range(2)] for band in range(2)]

    stack[...] = jnp.zeros_like(stack)
    load_start.wait()
    for chunk in range(CHUNKS):
        set_stack(chunk, start_fields(chunk), True)
    load_v.wait()
    pl.semaphore_wait(barrier, GROUPS + TILES - 2)

    def prepare_v(z):
        for over in range(XS):
            unpack(v_raw, v_ref, z * XS + over, over, lambda band, tile: rank_ref[band, tile, me_t])

    def prepare_u(z, carry):
        for over in range(XS):
            unpack(u_raw, u_ref, z * XS + over, over, lambda band, tile: rank_ref[band, me_t, tile])
        return carry

    send_codes(v_ref, 0, 0, prepare_v)
    for chunk in range(1, CHUNKS):
        send_codes(v_ref, chunk, chunk)

    load_trig.wait()
    limits = onset_ref[pl.ds(me_f % 2, 1), :]
    window = jnp.where(lax.broadcasted_iota(jnp.int32, (NT, HALF), 0) < limits, 1.0, 0.0).astype(BF16)
    sums = contract(trig_ref[...], window, 1, 0)
    table[...] = (sums[: 2 * TABLE] + sums[2 * TABLE : 4 * TABLE] + sums[4 * TABLE :]) * (1.0 / NT)
    for wave in range(NF):
        low, high = NF - 1 - wave, NF + 1 + wave
        cos_low = table[low : low + NF, :]
        cos_high = table[high : high + NF, :]
        sin_low = table[TABLE + low : TABLE + low + NF, :]
        sin_high = table[TABLE + high : TABLE + high + NF, :]
        gate_rows[2 * wave, 0] = cos_low + cos_high
        gate_rows[2 * wave, 1] = sin_high + sin_low
        gate_rows[2 * wave + 1, 0] = sin_high - sin_low
        gate_rows[2 * wave + 1, 1] = cos_low - cos_high
    load_u.wait()
    lax.fori_loop(0, ZS, prepare_u, 0)

    for half in range(HALVES):
        forward = half % 2 == 0
        for chunk in range(CHUNKS):
            phase = half * CHUNKS + chunk
            rows = slice(chunk * SC, (chunk + 1) * SC)
            image(u_ref if forward else v_ref, phase, forward)
            exchange(wave_out, wave_in, wave_send, wave_recv, phase)
            gate(phase)
            exchange(gated_out, gated_in, gated_send, gated_recv, phase)
            fields = gated_fields(phase)
            if not forward:
                begun = start_fields(chunk)
                fields = [[begun[band][part] + fields[band][part] for part in range(2)] for band in range(2)]
            if half + 1 < HALVES:
                set_stack(chunk, fields, not forward)
                send_codes(u_ref if forward else v_ref, phase + CHUNKS, chunk)
            if half >= HALVES - 2:
                target = up_ref if forward else focus_ref
                for band in range(2):
                    for part in range(2):
                        target[band, part, rows, :] = fields[band][part]
    for phase in range(PHASES):
        wait_bytes(code_out.at[phase, pl.ds(0, ROWS - RANK)], code_send.at[phase])
        wait_bytes(wave_out.at[phase, pl.ds(0, GROUPS - 1)], wave_send.at[phase])
        wait_bytes(gated_out.at[phase, pl.ds(0, GROUPS - 1)], gated_send.at[phase])


def per_device(trig, focus_start, v_factor, u_factor, tile_ranks, onsets):
    def split_lanes(factor):
        blocks = factor.reshape(2, TILES, RANK, 2, 2, HALF)
        return blocks.transpose(0, 1, 2, 4, 3, 5).reshape(2, TILES, 4 * RANK, HALF)

    vmem = pl.BlockSpec(memory_space=pltpu.VMEM)
    anywhere = pl.BlockSpec(memory_space=pl.ANY)
    dma = pltpu.SemaphoreType.DMA
    field = pltpu.VMEM((2, 2, S, TILE), F32)
    return pl.pallas_call(
        kernel,
        out_shape=(field, field),
        in_specs=[anywhere, anywhere, anywhere, pl.BlockSpec(memory_space=pltpu.SMEM), vmem, anywhere],
        out_specs=(vmem, vmem),
        scratch_shapes=[
            pltpu.VMEM((2, 2, S, TILE), F32),
            pltpu.VMEM((6 * TABLE, NT), BF16),
            pltpu.VMEM((2, TILES, 4 * RANK, HALF), BF16),
            pltpu.VMEM((2, TILES, 4 * RANK, HALF), BF16),
            pltpu.VMEM((2, ROWS, 2 * TILE), BF16),
            pltpu.VMEM((2, ROWS, 2 * TILE), BF16),
            pltpu.VMEM((XS, 2, 4 * RANK, HALF), F32),
            pltpu.VMEM((CHUNKS, 2, 4 * SC, 2 * TILE), BF16),
            pltpu.VMEM((PHASES, ROWS, 4 * SC), BF16),
            pltpu.VMEM((PHASES, ROWS, 4 * SC), BF16),
            pltpu.VMEM((4 * SC, ROWS), BF16),
            pltpu.VMEM((PHASES, GROUPS, 2, 16, HALF), BF16),
            pltpu.VMEM((PHASES, GROUPS, 2, 16, HALF), BF16),
            pltpu.VMEM((PHASES, GROUPS, 2, 16, HALF), BF16),
            pltpu.VMEM((PHASES, GROUPS, 2, 16, HALF), BF16),
            pltpu.VMEM((2 * TABLE, HALF), F32),
            pltpu.VMEM((2 * NF, 2, NF, HALF), F32),
            dma((4,)),
            dma((PHASES,)),
            dma((PHASES,)),
            dma((PHASES,)),
            dma((PHASES,)),
            dma((PHASES,)),
            dma((PHASES,)),
        ],
        compiler_params=pltpu.CompilerParams(collective_id=0, has_side_effects=True),
    )(
        focus_start,
        split_lanes(v_factor),
        split_lanes(u_factor),
        tile_ranks,
        onsets.reshape(2, HALF),
        trig,
    )


def solution(mesh):
    placed = (
        P("freq", None, None, "tile"),
        P("freq", None, "tile", None, None, None),
        P("freq", "tile", None, None, None, None),
        P("freq", None, None),
        P("tile"),
    )
    trig = trig_parts()

    def body(*args):
        return per_device(jnp.asarray(trig), *args)

    return jax.shard_map(
        body,
        mesh=mesh,
        in_specs=placed,
        out_specs=(P("freq", None, None, "tile"), P("freq", None, None, "tile")),
        check_vma=False,
    )
```

```python
import functools
import math

import jax
import jax.numpy as jnp
import ml_dtypes
import numpy as np
from jax import lax
from jax.experimental import pallas as pl
from jax.experimental.pallas import tpu as pltpu
from jax.sharding import PartitionSpec as P

TILE = 256
RANK = 64
S = 64
NT = 512
ITERS = 2
NF = 16
ZS = 8
XS = 4
TILES = ZS * XS
GROUPS = 8
CHUNKS = 2
SC = S // CHUNKS
HALVES = 2 * ITERS
PHASES = HALVES * CHUNKS
ROWS = TILES * RANK
HALF = TILE // 2
TABLE = 48
MESH = pl.DeviceIdType.MESH
F32 = jnp.float32
BF16 = jnp.bfloat16


def trig_parts():
    orders = np.arange(TABLE)[:, None] - (NF - 1)
    angles = (orders * np.arange(NT)[None, :] % NT) * (2.0 * math.pi / NT)
    rest = np.concatenate([np.cos(angles), np.sin(angles)], axis=0)
    parts = []
    for _ in range(3):
        part = rest.astype(ml_dtypes.bfloat16)
        parts.append(part)
        rest = rest - part.astype(np.float64)
    return np.concatenate(parts, axis=0)


def contract(left, right, left_dim, right_dim):
    return lax.dot_general(
        left, right, (((left_dim,), (right_dim,)), ((), ())), preferred_element_type=F32
    )


def kernel(
    start_hbm, v_hbm, u_hbm, rank_ref, onset_ref, trig_hbm,
    focus_ref, up_ref,
    start_ref, trig_ref, v_raw, u_raw, v_ref, u_ref, spread, stack, code_out, code_in, turned,
    wave_out, wave_in, gated_out, gated_in, table, gate_rows,
    load_sem, code_send, code_recv, wave_send, wave_recv, gated_send, gated_recv,
):
    me_f = lax.axis_index("freq")
    me_t = lax.axis_index("tile")
    me_z = me_t // XS
    me_x = me_t % XS

    barrier = pltpu.get_barrier_semaphore()
    for step in range(1, GROUPS):
        pl.semaphore_signal(
            barrier, inc=1, device_id=((me_f + step) % GROUPS, me_t), device_id_type=MESH
        )
    for step in range(1, TILES):
        pl.semaphore_signal(
            barrier, inc=1, device_id=(me_f, (me_t + step) % TILES), device_id_type=MESH
        )
    load_v = pltpu.make_async_copy(v_hbm, v_raw, load_sem.at[0])
    load_u = pltpu.make_async_copy(u_hbm, u_raw, load_sem.at[1])
    load_start = pltpu.make_async_copy(start_hbm, start_ref, load_sem.at[2])
    load_trig = pltpu.make_async_copy(trig_hbm, trig_ref, load_sem.at[3])
    for load in (load_start, load_v, load_trig, load_u):
        load.start()

    def set_stack(chunk, fields, forward):
        for band in range(2):
            real = fields[band][0].astype(BF16)
            imag = fields[band][1].astype(BF16)
            top = band * 2 * SC
            if forward:
                blocks = ((real, -imag), (imag, real))
            else:
                blocks = ((real, imag), (imag, -real))
            for part in range(2):
                rows = slice(top + part * SC, top + (part + 1) * SC)
                stack[chunk, band, rows, 0:TILE] = blocks[part][0]
                stack[chunk, band, rows, TILE : 2 * TILE] = blocks[part][1]

    def unpack(raw, factor_ref, tile, slot, rank_of):
        for band in range(2):
            live = lax.broadcasted_iota(jnp.int32, (RANK, HALF), 0) < rank_of(band, tile)
            spread[slot, band] = raw[band, tile].astype(F32)
            rows = pl.ds(pl.multiple_of(tile * RANK, RANK), RANK)
            for side in range(2):
                for part in range(2):
                    piece = spread[slot, band, pl.ds(2 * side + part, RANK, stride=4), :]
                    piece = jnp.where(live, piece, 0.0).astype(BF16)
                    left = part * TILE + side * HALF
                    factor_ref[band, rows, left : left + HALF] = piece

    def send_codes(factor_ref, phase, chunk, prepare=None):
        def pair(index, carry):
            planes = ((me_z + ZS // 2 - index) % ZS, (me_z + ZS // 2 + 1 + index) % ZS)
            for z in planes:
                if prepare is not None:
                    prepare(z)
                rows = pl.ds(pl.multiple_of(z * (XS * RANK), XS * RANK), XS * RANK)
                product = contract(factor_ref[0, rows, :], stack[chunk, 0], 1, 1) + contract(
                    factor_ref[1, rows, :], stack[chunk, 1], 1, 1
                )
                code_out[phase, rows, :] = product.astype(BF16)
            for over in (2, 1, 3, 0):
                for side, z in enumerate(planes):
                    tile = z * XS + (me_x + over) % XS

                    def start(tile=tile):
                        pltpu.make_async_remote_copy(
                            src_ref=code_out.at[phase, pl.ds(pl.multiple_of(tile * RANK, RANK), RANK)],
                            dst_ref=code_in.at[phase, pl.ds(pl.multiple_of(me_t * RANK, RANK), RANK)],
                            send_sem=code_send.at[phase],
                            recv_sem=code_recv.at[phase],
                            device_id=(me_f, tile),
                            device_id_type=MESH,
                        ).start()

                    if over or not side:
                        start()
                    else:
                        pl.when(index < ZS // 2 - 1)(start)
            return carry

        lax.fori_loop(0, ZS // 2, pair, 0)
        own = pl.ds(pl.multiple_of(me_t * RANK, RANK), RANK)
        code_in[phase, own, :] = code_out[phase, own, :]

    def wait_bytes(ref, sem):
        pltpu.make_async_copy(ref, ref, sem).wait()

    def image(factor_ref, phase, forward):
        wait_bytes(code_in.at[phase, pl.ds(0, ROWS - RANK)], code_recv.at[phase])
        turned[...] = code_in[phase].T
        sign = 1.0 if forward else -1.0
        for band in range(2):
            product = contract(
                turned[band * 2 * SC : (band + 1) * 2 * SC, :], factor_ref[band], 1, 0
            )
            real = product[:SC, :TILE] - sign * product[SC:, TILE:]
            imag = product[SC:, :TILE] + sign * product[:SC, TILE:]
            for group in range(GROUPS):
                rows = slice((group // 2) * 8, (group // 2 + 1) * 8)
                lanes = slice((group % 2) * HALF, (group % 2 + 1) * HALF)
                pair = jnp.concatenate([real[rows, lanes], imag[rows, lanes]], axis=0)
                wave_out[phase, group, band] = pair.astype(BF16)

    def exchange(source, target, send, recv, phase):
        for step in (4, 5, 3, 2, 6, 7, 1):
            peer = (me_f + step) % GROUPS
            pltpu.make_async_remote_copy(
                src_ref=source.at[phase, peer],
                dst_ref=target.at[phase, me_f],
                send_sem=send.at[phase],
                recv_sem=recv.at[phase],
                device_id=(peer, me_t),
                device_id_type=MESH,
            ).start()
        target[phase, me_f] = source[phase, me_f]
        wait_bytes(target.at[phase, pl.ds(0, GROUPS - 1)], recv.at[phase])

    def gate(phase):
        waves = []
        for index in range(NF):
            pair = wave_in[phase, index // 2, index % 2].astype(F32)
            waves.append((pair[:8], pair[8:]))

        def rows(index, carry):
            results = []
            for kind in range(2):
                totals = [None] * 4
                for wave in range(NF):
                    for part in range(2):
                        weight = gate_rows[2 * index + kind, part, wave : wave + 1, :]
                        term = weight * waves[wave][part]
                        lane = 2 * (wave % 2) + part
                        totals[lane] = term if totals[lane] is None else totals[lane] + term
                results.append((totals[0] + totals[1]) + (totals[2] + totals[3]))
            gated_out[phase, index // 2, index % 2] = jnp.concatenate(results, axis=0).astype(BF16)
            return carry

        lax.fori_loop(0, NF, rows, 0)

    def gated_fields(phase):
        def field(band, part):
            part_rows = slice(part * 8, part * 8 + 8)
            bands = [
                jnp.concatenate(
                    [gated_in[phase, 2 * up + side, band].astype(F32)[part_rows] for side in range(2)], axis=1
                )
                for up in range(GROUPS // 2)
            ]
            return jnp.concatenate(bands, axis=0)

        return [[field(band, part) for part in range(2)] for band in range(2)]

    def start_fields(chunk):
        rows = slice(chunk * SC, (chunk + 1) * SC)
        return [[start_ref[band, part, rows, :] for part in range(2)] for band in range(2)]

    stack[...] = jnp.zeros_like(stack)
    load_start.wait()
    for chunk in range(CHUNKS):
        set_stack(chunk, start_fields(chunk), True)
    load_v.wait()
    pl.semaphore_wait(barrier, GROUPS + TILES - 2)

    def prepare_v(z):
        for over in range(XS):
            unpack(v_raw, v_ref, z * XS + over, over, lambda band, tile: rank_ref[band, tile, me_t])

    def prepare_u(z, carry):
        for over in range(XS):
            unpack(u_raw, u_ref, z * XS + over, over, lambda band, tile: rank_ref[band, me_t, tile])
        return carry

    send_codes(v_ref, 0, 0, prepare_v)
    for chunk in range(1, CHUNKS):
        send_codes(v_ref, chunk, chunk)

    load_trig.wait()
    limits = onset_ref[pl.ds(me_f % 2, 1), :]
    window = jnp.where(lax.broadcasted_iota(jnp.int32, (NT, HALF), 0) < limits, 1.0, 0.0).astype(BF16)
    sums = contract(trig_ref[...], window, 1, 0)
    table[...] = (sums[: 2 * TABLE] + sums[2 * TABLE : 4 * TABLE] + sums[4 * TABLE :]) * (1.0 / NT)
    for wave in range(NF):
        low, high = NF - 1 - wave, NF + 1 + wave
        cos_low = table[low : low + NF, :]
        cos_high = table[high : high + NF, :]
        sin_low = table[TABLE + low : TABLE + low + NF, :]
        sin_high = table[TABLE + high : TABLE + high + NF, :]
        gate_rows[2 * wave, 0] = cos_low + cos_high
        gate_rows[2 * wave, 1] = sin_high + sin_low
        gate_rows[2 * wave + 1, 0] = sin_high - sin_low
        gate_rows[2 * wave + 1, 1] = cos_low - cos_high
    load_u.wait()
    lax.fori_loop(0, ZS, prepare_u, 0)

    for half in range(HALVES):
        forward = half % 2 == 0
        for chunk in range(CHUNKS):
            phase = half * CHUNKS + chunk
            rows = slice(chunk * SC, (chunk + 1) * SC)
            image(u_ref if forward else v_ref, phase, forward)
            exchange(wave_out, wave_in, wave_send, wave_recv, phase)
            gate(phase)
            exchange(gated_out, gated_in, gated_send, gated_recv, phase)
            fields = gated_fields(phase)
            if not forward:
                begun = start_fields(chunk)
                fields = [[begun[band][part] + fields[band][part] for part in range(2)] for band in range(2)]
            if half + 1 < HALVES:
                set_stack(chunk, fields, not forward)
                send_codes(u_ref if forward else v_ref, phase + CHUNKS, chunk)
            if half >= HALVES - 2:
                target = up_ref if forward else focus_ref
                for band in range(2):
                    for part in range(2):
                        target[band, part, rows, :] = fields[band][part]
    for phase in range(PHASES):
        wait_bytes(code_out.at[phase, pl.ds(0, ROWS - RANK)], code_send.at[phase])
        wait_bytes(wave_out.at[phase, pl.ds(0, GROUPS - 1)], wave_send.at[phase])
        wait_bytes(gated_out.at[phase, pl.ds(0, GROUPS - 1)], gated_send.at[phase])


def per_device(trig, focus_start, v_factor, u_factor, tile_ranks, onsets):
    def split_lanes(factor):
        blocks = factor.reshape(2, TILES, RANK, 2, 2, HALF)
        return blocks.transpose(0, 1, 2, 4, 3, 5).reshape(2, TILES, 4 * RANK, HALF)

    vmem = pl.BlockSpec(memory_space=pltpu.VMEM)
    anywhere = pl.BlockSpec(memory_space=pl.ANY)
    dma = pltpu.SemaphoreType.DMA
    field = pltpu.VMEM((2, 2, S, TILE), F32)
    return pl.pallas_call(
        kernel,
        out_shape=(field, field),
        in_specs=[anywhere, anywhere, anywhere, pl.BlockSpec(memory_space=pltpu.SMEM), vmem, anywhere],
        out_specs=(vmem, vmem),
        scratch_shapes=[
            pltpu.VMEM((2, 2, S, TILE), F32),
            pltpu.VMEM((6 * TABLE, NT), BF16),
            pltpu.VMEM((2, TILES, 4 * RANK, HALF), BF16),
            pltpu.VMEM((2, TILES, 4 * RANK, HALF), BF16),
            pltpu.VMEM((2, ROWS, 2 * TILE), BF16),
            pltpu.VMEM((2, ROWS, 2 * TILE), BF16),
            pltpu.VMEM((XS, 2, 4 * RANK, HALF), F32),
            pltpu.VMEM((CHUNKS, 2, 4 * SC, 2 * TILE), BF16),
            pltpu.VMEM((PHASES, ROWS, 4 * SC), BF16),
            pltpu.VMEM((PHASES, ROWS, 4 * SC), BF16),
            pltpu.VMEM((4 * SC, ROWS), BF16),
            pltpu.VMEM((PHASES, GROUPS, 2, 16, HALF), BF16),
            pltpu.VMEM((PHASES, GROUPS, 2, 16, HALF), BF16),
            pltpu.VMEM((PHASES, GROUPS, 2, 16, HALF), BF16),
            pltpu.VMEM((PHASES, GROUPS, 2, 16, HALF), BF16),
            pltpu.VMEM((2 * TABLE, HALF), F32),
            pltpu.VMEM((2 * NF, 2, NF, HALF), F32),
            dma((4,)),
            dma((PHASES,)),
            dma((PHASES,)),
            dma((PHASES,)),
            dma((PHASES,)),
            dma((PHASES,)),
            dma((PHASES,)),
        ],
        compiler_params=pltpu.CompilerParams(collective_id=0, has_side_effects=True),
    )(
        focus_start,
        split_lanes(v_factor),
        split_lanes(u_factor),
        tile_ranks,
        onsets.reshape(2, HALF),
        trig,
    )


def solution(mesh):
    placed = (
        P("freq", None, None, "tile"),
        P("freq", None, "tile", None, None, None),
        P("freq", "tile", None, None, None, None),
        P("freq", None, None),
        P("tile"),
    )
    trig = trig_parts()

    def body(*args):
        return per_device(jnp.asarray(trig), *args)

    return jax.shard_map(
        body,
        mesh=mesh,
        in_specs=placed,
        out_specs=(P("freq", None, None, "tile"), P("freq", None, None, "tile")),
        check_vma=False,
    )
```

```python
import functools
import math

import jax
import jax.numpy as jnp
import ml_dtypes
import numpy as np
from jax import lax
from jax.experimental import pallas as pl
from jax.experimental.pallas import tpu as pltpu
from jax.sharding import PartitionSpec as P

TILE = 256
RANK = 64
S = 64
NT = 512
ITERS = 2
NF = 16
ZS = 8
XS = 4
TILES = ZS * XS
GROUPS = 8
CHUNKS = 2
SC = S // CHUNKS
HALVES = 2 * ITERS
PHASES = HALVES * CHUNKS
ROWS = TILES * RANK
HALF = TILE // 2
TABLE = 48
MESH = pl.DeviceIdType.MESH
F32 = jnp.float32
BF16 = jnp.bfloat16


def trig_parts():
    orders = np.arange(TABLE)[:, None] - (NF - 1)
    angles = (orders * np.arange(NT)[None, :] % NT) * (2.0 * math.pi / NT)
    rest = np.concatenate([np.cos(angles), np.sin(angles)], axis=0)
    parts = []
    for _ in range(3):
        part = rest.astype(ml_dtypes.bfloat16)
        parts.append(part)
        rest = rest - part.astype(np.float64)
    return np.concatenate(parts, axis=0)


def contract(left, right, left_dim, right_dim):
    return lax.dot_general(
        left, right, (((left_dim,), (right_dim,)), ((), ())), preferred_element_type=F32
    )


def kernel(
    start_hbm, v_hbm, u_hbm, rank_ref, onset_ref, trig_hbm,
    focus_ref, up_ref,
    start_ref, trig_ref, v_raw, u_raw, v_ref, u_ref, spread, stack, code_out, code_in,
    wave_out, wave_in, gated_out, gated_in, table, gate_rows,
    load_sem, code_send, code_recv, wave_send, wave_recv, gated_send, gated_recv,
):
    me_f = lax.axis_index("freq")
    me_t = lax.axis_index("tile")
    me_z = me_t // XS
    me_x = me_t % XS

    barrier = pltpu.get_barrier_semaphore()
    for step in range(1, GROUPS):
        pl.semaphore_signal(
            barrier, inc=1, device_id=((me_f + step) % GROUPS, me_t), device_id_type=MESH
        )
    for step in range(1, TILES):
        pl.semaphore_signal(
            barrier, inc=1, device_id=(me_f, (me_t + step) % TILES), device_id_type=MESH
        )
    load_v = pltpu.make_async_copy(v_hbm, v_raw, load_sem.at[0])
    load_u = pltpu.make_async_copy(u_hbm, u_raw, load_sem.at[1])
    load_start = pltpu.make_async_copy(start_hbm, start_ref, load_sem.at[2])
    load_trig = pltpu.make_async_copy(trig_hbm, trig_ref, load_sem.at[3])
    for load in (load_start, load_v, load_trig):
        load.start()

    def set_stack(chunk, fields, forward):
        for band in range(2):
            real = fields[band][0].astype(BF16)
            imag = fields[band][1].astype(BF16)
            top = band * 2 * SC
            if forward:
                blocks = ((real, -imag), (imag, real))
            else:
                blocks = ((real, imag), (imag, -real))
            for part in range(2):
                rows = slice(top + part * SC, top + (part + 1) * SC)
                stack[chunk, band, rows, 0:TILE] = blocks[part][0]
                stack[chunk, band, rows, TILE : 2 * TILE] = blocks[part][1]

    def unpack(raw, factor_ref, tile, slot, rank_of):
        for band in range(2):
            live = lax.broadcasted_iota(jnp.int32, (RANK, HALF), 0) < rank_of(band, tile)
            spread[slot, band] = raw[band, tile].astype(F32)
            rows = pl.ds(pl.multiple_of(tile * RANK, RANK), RANK)
            for side in range(2):
                for part in range(2):
                    piece = spread[slot, band, pl.ds(2 * side + part, RANK, stride=4), :]
                    piece = jnp.where(live, piece, 0.0).astype(BF16)
                    left = part * TILE + side * HALF
                    factor_ref[band, rows, left : left + HALF] = piece

    def send_codes(factor_ref, phase, chunk):
        def pair(index, carry):
            planes = ((me_z + ZS // 2 - index) % ZS, (me_z + ZS // 2 + 1 + index) % ZS)
            for z in planes:
                rows = pl.ds(pl.multiple_of(z * (XS * RANK), XS * RANK), XS * RANK)
                product = contract(factor_ref[0, rows, :], stack[chunk, 0], 1, 1) + contract(
                    factor_ref[1, rows, :], stack[chunk, 1], 1, 1
                )
                code_out[phase, rows, :] = product.astype(BF16)
            for over in (2, 1, 3, 0):
                for side, z in enumerate(planes):
                    tile = z * XS + (me_x + over) % XS

                    def start(tile=tile):
                        pltpu.make_async_remote_copy(
                            src_ref=code_out.at[phase, pl.ds(pl.multiple_of(tile * RANK, RANK), RANK)],
                            dst_ref=code_in.at[phase, pl.ds(pl.multiple_of(me_t * RANK, RANK), RANK)],
                            send_sem=code_send.at[phase],
                            recv_sem=code_recv.at[phase, index],
                            device_id=(me_f, tile),
                            device_id_type=MESH,
                        ).start()

                    if over or not side:
                        start()
                    else:
                        pl.when(index < ZS // 2 - 1)(start)
            return carry

        lax.fori_loop(0, ZS // 2, pair, 0)
        own = pl.ds(pl.multiple_of(me_t * RANK, RANK), RANK)
        code_in[phase, own, :] = code_out[phase, own, :]

    def wait_bytes(ref, sem):
        pltpu.make_async_copy(ref, ref, sem).wait()

    def image(factor_ref, phase, forward):
        totals = [None, None]
        for index in range(ZS // 2):
            blocks = 2 * XS - (1 if index == ZS // 2 - 1 else 0)
            wait_bytes(code_in.at[phase, pl.ds(0, blocks * RANK)], code_recv.at[phase, index])
            for z in ((me_z + ZS // 2 + index) % ZS, (me_z + ZS // 2 - 1 - index) % ZS):
                rows = pl.ds(pl.multiple_of(z * (XS * RANK), XS * RANK), XS * RANK)
                turned = code_in[phase, rows, :].T
                for band in range(2):
                    term = contract(
                        turned[band * 2 * SC : (band + 1) * 2 * SC, :], factor_ref[band, rows, :], 1, 0
                    )
                    totals[band] = term if totals[band] is None else totals[band] + term
        sign = 1.0 if forward else -1.0
        for band in range(2):
            product = totals[band]
            real = product[:SC, :TILE] - sign * product[SC:, TILE:]
            imag = product[SC:, :TILE] + sign * product[:SC, TILE:]
            for group in range(GROUPS):
                rows = slice((group // 2) * 8, (group // 2 + 1) * 8)
                lanes = slice((group % 2) * HALF, (group % 2 + 1) * HALF)
                pair = jnp.concatenate([real[rows, lanes], imag[rows, lanes]], axis=0)
                wave_out[phase, group, band] = pair.astype(BF16)

    def exchange(source, target, send, recv, phase):
        for step in (4, 5, 3, 2, 6, 7, 1):
            peer = (me_f + step) % GROUPS
            pltpu.make_async_remote_copy(
                src_ref=source.at[phase, peer],
                dst_ref=target.at[phase, me_f],
                send_sem=send.at[phase],
                recv_sem=recv.at[phase],
                device_id=(peer, me_t),
                device_id_type=MESH,
            ).start()
        target[phase, me_f] = source[phase, me_f]
        wait_bytes(target.at[phase, pl.ds(0, GROUPS - 1)], recv.at[phase])

    def gate(phase):
        waves = []
        for index in range(NF):
            pair = wave_in[phase, index // 2, index % 2].astype(F32)
            waves.append((pair[:8], pair[8:]))

        def rows(index, carry):
            results = []
            for kind in range(2):
                totals = [None] * 4
                for wave in range(NF):
                    for part in range(2):
                        weight = gate_rows[2 * index + kind, part, wave : wave + 1, :]
                        term = weight * waves[wave][part]
                        lane = 2 * (wave % 2) + part
                        totals[lane] = term if totals[lane] is None else totals[lane] + term
                results.append((totals[0] + totals[1]) + (totals[2] + totals[3]))
            gated_out[phase, index // 2, index % 2] = jnp.concatenate(results, axis=0).astype(BF16)
            return carry

        lax.fori_loop(0, NF, rows, 0)

    def gated_fields(phase):
        def field(band, part):
            part_rows = slice(part * 8, part * 8 + 8)
            bands = [
                jnp.concatenate(
                    [gated_in[phase, 2 * up + side, band].astype(F32)[part_rows] for side in range(2)], axis=1
                )
                for up in range(GROUPS // 2)
            ]
            return jnp.concatenate(bands, axis=0)

        return [[field(band, part) for part in range(2)] for band in range(2)]

    def start_fields(chunk):
        rows = slice(chunk * SC, (chunk + 1) * SC)
        return [[start_ref[band, part, rows, :] for part in range(2)] for band in range(2)]

    def prepare_v(z, carry):
        for over in range(XS):
            unpack(v_raw, v_ref, z * XS + over, over, lambda band, tile: rank_ref[band, tile, me_t])
        return carry

    stack[...] = jnp.zeros_like(stack)
    load_start.wait()
    for chunk in range(CHUNKS):
        set_stack(chunk, start_fields(chunk), True)
    load_v.wait()
    load_u.start()
    lax.fori_loop(0, ZS, prepare_v, 0)
    pl.semaphore_wait(barrier, GROUPS + TILES - 2)

    def prepare_u(z, carry):
        for over in range(XS):
            unpack(u_raw, u_ref, z * XS + over, over, lambda band, tile: rank_ref[band, me_t, tile])
        return carry

    for chunk in range(CHUNKS):
        send_codes(v_ref, chunk, chunk)

    load_trig.wait()
    limits = onset_ref[pl.ds(me_f % 2, 1), :]
    window = jnp.where(lax.broadcasted_iota(jnp.int32, (NT, HALF), 0) < limits, 1.0, 0.0).astype(BF16)
    sums = contract(trig_ref[...], window, 1, 0)
    table[...] = (sums[: 2 * TABLE] + sums[2 * TABLE : 4 * TABLE] + sums[4 * TABLE :]) * (1.0 / NT)
    for wave in range(NF):
        low, high = NF - 1 - wave, NF + 1 + wave
        cos_low = table[low : low + NF, :]
        cos_high = table[high : high + NF, :]
        sin_low = table[TABLE + low : TABLE + low + NF, :]
        sin_high = table[TABLE + high : TABLE + high + NF, :]
        gate_rows[2 * wave, 0] = cos_low + cos_high
        gate_rows[2 * wave, 1] = sin_high + sin_low
        gate_rows[2 * wave + 1, 0] = sin_high - sin_low
        gate_rows[2 * wave + 1, 1] = cos_low - cos_high
    load_u.wait()
    lax.fori_loop(0, ZS, prepare_u, 0)

    for half in range(HALVES):
        forward = half % 2 == 0
        for chunk in range(CHUNKS):
            phase = half * CHUNKS + chunk
            rows = slice(chunk * SC, (chunk + 1) * SC)
            image(u_ref if forward else v_ref, phase, forward)
            exchange(wave_out, wave_in, wave_send, wave_recv, phase)
            gate(phase)
            exchange(gated_out, gated_in, gated_send, gated_recv, phase)
            fields = gated_fields(phase)
            if not forward:
                begun = start_fields(chunk)
                fields = [[begun[band][part] + fields[band][part] for part in range(2)] for band in range(2)]
            if half + 1 < HALVES:
                set_stack(chunk, fields, not forward)
                send_codes(u_ref if forward else v_ref, phase + CHUNKS, chunk)
            if half >= HALVES - 2:
                target = up_ref if forward else focus_ref
                for band in range(2):
                    for part in range(2):
                        target[band, part, rows, :] = fields[band][part]
    for phase in range(PHASES):
        wait_bytes(code_out.at[phase, pl.ds(0, ROWS - RANK)], code_send.at[phase])
        wait_bytes(wave_out.at[phase, pl.ds(0, GROUPS - 1)], wave_send.at[phase])
        wait_bytes(gated_out.at[phase, pl.ds(0, GROUPS - 1)], gated_send.at[phase])


def per_device(trig, focus_start, v_factor, u_factor, tile_ranks, onsets):
    def split_lanes(factor):
        blocks = factor.reshape(2, TILES, RANK, 2, 2, HALF)
        return blocks.transpose(0, 1, 2, 4, 3, 5).reshape(2, TILES, 4 * RANK, HALF)

    vmem = pl.BlockSpec(memory_space=pltpu.VMEM)
    anywhere = pl.BlockSpec(memory_space=pl.ANY)
    dma = pltpu.SemaphoreType.DMA
    field = pltpu.VMEM((2, 2, S, TILE), F32)
    return pl.pallas_call(
        kernel,
        out_shape=(field, field),
        in_specs=[anywhere, anywhere, anywhere, pl.BlockSpec(memory_space=pltpu.SMEM), vmem, anywhere],
        out_specs=(vmem, vmem),
        scratch_shapes=[
            pltpu.VMEM((2, 2, S, TILE), F32),
            pltpu.VMEM((6 * TABLE, NT), BF16),
            pltpu.VMEM((2, TILES, 4 * RANK, HALF), BF16),
            pltpu.VMEM((2, TILES, 4 * RANK, HALF), BF16),
            pltpu.VMEM((2, ROWS, 2 * TILE), BF16),
            pltpu.VMEM((2, ROWS, 2 * TILE), BF16),
            pltpu.VMEM((XS, 2, 4 * RANK, HALF), F32),
            pltpu.VMEM((CHUNKS, 2, 4 * SC, 2 * TILE), BF16),
            pltpu.VMEM((PHASES, ROWS, 4 * SC), BF16),
            pltpu.VMEM((PHASES, ROWS, 4 * SC), BF16),
            pltpu.VMEM((PHASES, GROUPS, 2, 16, HALF), BF16),
            pltpu.VMEM((PHASES, GROUPS, 2, 16, HALF), BF16),
            pltpu.VMEM((PHASES, GROUPS, 2, 16, HALF), BF16),
            pltpu.VMEM((PHASES, GROUPS, 2, 16, HALF), BF16),
            pltpu.VMEM((2 * TABLE, HALF), F32),
            pltpu.VMEM((2 * NF, 2, NF, HALF), F32),
            dma((4,)),
            dma((PHASES,)),
            dma((PHASES, ZS // 2)),
            dma((PHASES,)),
            dma((PHASES,)),
            dma((PHASES,)),
            dma((PHASES,)),
        ],
        compiler_params=pltpu.CompilerParams(collective_id=0, has_side_effects=True),
    )(
        focus_start,
        split_lanes(v_factor),
        split_lanes(u_factor),
        tile_ranks,
        onsets.reshape(2, HALF),
        trig,
    )


def solution(mesh):
    placed = (
        P("freq", None, None, "tile"),
        P("freq", None, "tile", None, None, None),
        P("freq", "tile", None, None, None, None),
        P("freq", None, None),
        P("tile"),
    )
    trig = trig_parts()

    def body(*args):
        return per_device(jnp.asarray(trig), *args)

    return jax.shard_map(
        body,
        mesh=mesh,
        in_specs=placed,
        out_specs=(P("freq", None, None, "tile"), P("freq", None, None, "tile")),
        check_vma=False,
    )
```
